32 devices in a mesh: groups: 2 (over y), seq: 4 (over z), section: 2 (over x), tp: 2 (over core).
Axes of the slice: x: 2, y: 2, z: 4, core: 2. Of those that a mesh axis runs over, the one named last changes fastest.
Arguments:
- hidden_in: bfloat16 [16, 8192], P('groups', ('seq', 'section', 'tp')), parts along dimension 0, may hold values from -6 to 6
- lengths: int32 [16], P('groups'), parts along dimension 0, may hold values from 1 to 512, as said below
- key_value_cache: bfloat16 [16, 2, 512, 1024], P('groups', None, 'seq', ('section', 'tp')), parts along dimension 0, may hold values from -900 to 900
- attn_gain: float32 [8192], P('seq'), may hold values from 0.1 to 1.9
- w_query: bfloat16 [8192, 8192], P('seq', ('section', 'tp')), may hold values from -0.0625 to 0.0625
- key_value_weight: bfloat16 [8192, 2, 1024], P('seq', None, ('section', 'tp')), may hold values from -0.0625 to 0.0625
- w_output: bfloat16 [8192, 8192], P(('section', 'tp'), 'seq'), may hold values from -0.0625 to 0.0625
- mamba_gain: float32 [8192], P('seq'), may hold values from 0.1 to 1.9
- w_inproj: bfloat16 [8192, 2, 16384], P('seq', None, ('section', 'tp')), may hold values from -0.09375 to 0.09375
- conv_weight: float32 [4, 16384], P(None, ('section', 'tp', 'seq')), may hold values from -3 to 3
- conv_bias: float32 [16384], P(('section', 'tp', 'seq')), may hold values from -3 to 3
- w_xproj: bfloat16 [16384, 544], P(('section', 'tp', 'seq')), may hold values from -0.046875 to 0.046875
- w_dtproj: bfloat16 [512, 16384], P(None, ('section', 'tp', 'seq')), may hold values from -0.25 to 0.25
- dt_bias: float32 [16384], P(('section', 'tp', 'seq')), may hold values from -4 to 0
- a_log: float32 [16, 16384], P(None, ('section', 'tp', 'seq')), may hold values from 0 to 2.77
- d_skip: float32 [16384], P(('section', 'tp', 'seq')), may hold values from 0.25 to 2
- w_outproj: bfloat16 [16384, 8192], P(('section', 'tp'), 'seq'), may hold values from -0.046875 to 0.046875
- ssm_state: float32 [16, 16, 16384], P('groups', None, ('section', 'tp', 'seq')), parts along dimension 0, may hold values from -6 to 6
- conv_window: bfloat16 [16, 3, 16384], P('groups', None, ('section', 'tp', 'seq')), parts along dimension 0, may hold values from -6 to 6
Outputs:
- hidden_out: bfloat16 [16, 8192], P('groups', ('seq', 'section', 'tp')), parts along dimension 0
- state_out: float32 [16, 16, 16384], P('groups', None, ('section', 'tp', 'seq')), parts along dimension 0
- window_out: bfloat16 [16, 3, 16384], P('groups', None, ('section', 'tp', 'seq')), parts along dimension 0
The draws below stay inside these ranges and needn't reach their ends.
There are 2 independent parts, one for each index of `groups`. The reference program is written for one: setup_inputs(seed, part) draws one part's arguments, and reference() takes and returns one part's arrays. A program takes and returns all parts, laid end to end along the dimension named above; an argument that names none is the same for every part. Nothing has to cross between parts.
Inputs may be any that keep to these rules, and one draw needn't show every extreme that they name: `lengths`: the new token sits after the cached positions; one sequence of every draw has exactly 512; where there are two or more sequences, one or two others have at most 16.
All inputs are finite; a program needn't handle non-finite values.
Results may differ from the reference program's by a relative error of at most 0.012.
Values may be sent and summed in bfloat16 or wider, within the bound.
No kernel may reach another device: no remote copies, remote signals or barrier semaphores. Data moves between devices by JAX's collectives and lax.ppermute only.
A program may use at most 192 MiB of HBM per device.

```python
import jax
import jax.numpy as jnp
from jax import lax

MODEL_WIDTH = 8192
QUERY_HEADS = 64
KEY_VALUE_HEADS = 8
HEAD_SIZE = 128
DI = 16384
DS = 16
DCONV = 4
DTR = 512
BATCH_SEQUENCES = 8
CACHED_PER_INDEX = 128
CTX = 512
N_SEQ = 4


def sequence_ranks(key):
    order = jax.random.permutation(jax.random.fold_in(key, 5), BATCH_SEQUENCES)
    return jnp.argsort(order).astype(jnp.int32)


def draw_lengths(key, part):
    first_key, second_key, third_key = jax.random.split(jax.random.fold_in(key, 7), 3)
    ranks = sequence_ranks(key)
    missing = jax.random.randint(first_key, (BATCH_SEQUENCES,), 0, CTX)
    shifts = jax.random.randint(second_key, (BATCH_SEQUENCES,), 0, 4)
    counts = CTX - missing // jnp.left_shift(jnp.ones((BATCH_SEQUENCES,), jnp.int32), shifts)
    short_len = jax.random.randint(third_key, (BATCH_SEQUENCES,), 1, min(16, CTX) + 1)
    chosen = jnp.where(ranks <= 2, short_len, counts)
    return jnp.where(ranks == 0, CTX, chosen).astype(jnp.int32)


def draw_key_value_cache(key, part):
    noise_key = jax.random.fold_in(jax.random.fold_in(key, 11), 0)
    width_total = KEY_VALUE_HEADS * HEAD_SIZE
    base_draw = jnp.clip(jax.random.normal(noise_key, (BATCH_SEQUENCES, 2, CTX, width_total), jnp.float32), -6.0, 6.0)
    factor = jnp.array([1.5, 1.0], jnp.float32)[None, :, None, None]
    values = base_draw * factor
    return values.astype(jnp.bfloat16)


def raised(result, stream_key, source, target, parts, factor):
    def block_of(axis_at):
        return (jnp.arange(result.shape[axis_at]) // (result.shape[axis_at] // parts)).reshape((-1,) + (1,) * (result.ndim - 1 - axis_at))

    one_side = jax.random.permutation(stream_key, parts)[block_of(target)]
    second = (block_of(target) + parts // 2) % parts
    return jnp.where((block_of(source) == one_side) | (block_of(source) == second), factor * result, result)


def levels(own_key, extent, shards, least, top_value):
    factor_of, own = 1.0, jax.random.fold_in(own_key, 6)
    for dim, parts in shards:
        steps = jnp.exp(jax.random.uniform(jax.random.fold_in(own, dim), (parts,), jnp.float32, least / len(shards), top_value / len(shards)))
        factor_of = factor_of * jnp.repeat(steps, extent[dim] // parts).reshape([-1 if axis == dim else 1 for axis in range(len(extent))])
    return factor_of


def normal_values(rng, extent, scale, most, pieces=(), held_as=jnp.bfloat16):
    drawn = jax.random.normal(rng, extent, jnp.float32) * scale
    if len(pieces) > 0:
        drawn = levels(rng, extent, pieces, -0.22, 0.18) * drawn
    return jnp.clip(drawn, min=-most, max=most).astype(held_as)


def heavy_noise(rng, extent, scale, reach, shards, heavy, held_as=jnp.bfloat16):
    values = scale * jax.random.normal(rng, extent, jnp.float32)
    if shards:
        values = values * levels(rng, extent, shards, -0.22, 0.18)
    return jnp.clip(raised(values, jax.random.fold_in(rng, 3), *heavy), -reach, reach).astype(held_as)


def setup_inputs(seed: int = 0, part: int = 0) -> dict:
    key_of = jax.random.split(jax.random.key(seed), 20)
    part_keys = jax.random.split(jax.random.fold_in(key_of[19], part), 20)
    hidden_in = normal_values(part_keys[0], (BATCH_SEQUENCES, MODEL_WIDTH), 1.0, 6.0, ((1, 16),))
    lengths = draw_lengths(jax.random.fold_in(jax.random.fold_in(key_of[19], part), 71), part)
    key_value_cache = draw_key_value_cache(jax.random.fold_in(jax.random.fold_in(key_of[19], part), 71), part)
    attn_gain = jnp.clip(1.0 + 0.18 * jax.random.normal(key_of[3], (MODEL_WIDTH,), jnp.float32), 0.1, 1.9)
    w_query = normal_values(key_of[4], (MODEL_WIDTH, QUERY_HEADS * HEAD_SIZE), MODEL_WIDTH ** -0.5, 0.0625, ((0, 4), (1, 4)))
    key_value_weight = normal_values(key_of[5], (MODEL_WIDTH, 2, KEY_VALUE_HEADS * HEAD_SIZE), MODEL_WIDTH ** -0.5, 0.0625, ((0, 4), (2, 4)))
    w_output = normal_values(key_of[6], (QUERY_HEADS * HEAD_SIZE, MODEL_WIDTH), (QUERY_HEADS * HEAD_SIZE) ** -0.5, 0.0625, ((0, 4), (1, 4)))
    mamba_gain = jnp.clip(1.0 + 0.18 * jax.random.normal(key_of[7], (MODEL_WIDTH,), jnp.float32), 0.1, 1.9)
    w_inproj = heavy_noise(key_of[8], (MODEL_WIDTH, 2, DI), MODEL_WIDTH ** -0.5, 0.09375, ((0, 4), (2, 4)), (0, 2, 4, 2.0))
    conv_weight = normal_values(key_of[9], (DCONV, DI), 0.5, 3.0, ((1, 16),), jnp.float32)
    conv_bias = normal_values(key_of[10], (DI,), 0.5, 3.0, ((0, 16),), jnp.float32)
    w_xproj = normal_values(key_of[11], (DI, DTR + 2 * DS), DI ** -0.5, 0.046875, ((0, 16),))
    w_dtproj = normal_values(key_of[12], (DTR, DI), DTR ** -0.5, 0.25, ((1, 16),))
    dt_bias = jnp.clip(-4.0 + 4.0 * jax.random.uniform(key_of[13], (DI,), jnp.float32) ** levels(key_of[13], (DI,), ((0, 16),), -0.2, 0.2), -4.0, 0.0)
    a_log = jnp.clip(2.77 * jax.random.uniform(key_of[14], (DS, DI), jnp.float32) ** levels(key_of[14], (DS, DI), ((1, 16),), -0.2, 0.2), 0.0, 2.77)
    d_skip = jnp.clip(0.25 + 1.75 * jax.random.uniform(key_of[15], (DI,), jnp.float32) ** levels(key_of[15], (DI,), ((0, 16),), -0.2, 0.2), 0.25, 2.0)
    w_outproj = normal_values(key_of[16], (DI, MODEL_WIDTH), DI ** -0.5, 0.046875, ((0, 4), (1, 4)))
    ssm_state = normal_values(part_keys[17], (BATCH_SEQUENCES, DS, DI), 1.0, 6.0, ((2, 16),), jnp.float32)
    conv_window = normal_values(part_keys[18], (BATCH_SEQUENCES, DCONV - 1, DI), 1.0, 6.0, ((2, 16),))
    return dict(hidden_in=hidden_in, lengths=lengths, key_value_cache=key_value_cache, attn_gain=attn_gain, w_query=w_query, key_value_weight=key_value_weight, w_output=w_output, mamba_gain=mamba_gain, w_inproj=w_inproj, conv_weight=conv_weight, conv_bias=conv_bias, w_xproj=w_xproj, w_dtproj=w_dtproj, dt_bias=dt_bias, a_log=a_log, d_skip=d_skip, w_outproj=w_outproj, ssm_state=ssm_state, conv_window=conv_window)


EPSILON = 1e-06
NEGATIVE = -1e+30

def rounded(value):
    return lax.optimization_barrier(value.astype(jnp.bfloat16)).astype(jnp.float32)

def reference(hidden_in, lengths, key_value_cache, attn_gain, w_query, key_value_weight, w_output, mamba_gain, w_inproj, conv_weight, conv_bias, w_xproj, w_dtproj, dt_bias, a_log, d_skip, w_outproj, ssm_state, conv_window):
    query_groups_count = QUERY_HEADS // KEY_VALUE_HEADS
    hidden_wide = hidden_in.astype(jnp.float32)
    reciprocal_leading = lax.rsqrt(lax.optimization_barrier(jnp.mean(hidden_wide * hidden_wide, axis=1)) + EPSILON)
    normed_input = (hidden_wide * attn_gain).astype(jnp.bfloat16)
    query_rows_local = (reciprocal_leading[:, None] * jnp.dot(normed_input, w_query, preferred_element_type=jnp.float32)).astype(jnp.bfloat16)
    query_rows_local = query_rows_local.reshape(BATCH_SEQUENCES, KEY_VALUE_HEADS, query_groups_count, HEAD_SIZE).astype(jnp.float32)
    key_value_rows = reciprocal_leading[:, None] * jnp.dot(normed_input, key_value_weight.reshape(MODEL_WIDTH, 2 * KEY_VALUE_HEADS * HEAD_SIZE), preferred_element_type=jnp.float32)
    key_value_rows = key_value_rows.astype(jnp.bfloat16).reshape(BATCH_SEQUENCES, 2, KEY_VALUE_HEADS, HEAD_SIZE).astype(jnp.float32)
    new_key = key_value_rows[:, 0]
    new_value = key_value_rows[:, 1]
    inv_root = HEAD_SIZE ** (-0.5)
    stored_keys = key_value_cache[:, 0].reshape(BATCH_SEQUENCES, N_SEQ, CACHED_PER_INDEX, KEY_VALUE_HEADS, HEAD_SIZE).astype(jnp.float32)
    stored_values = key_value_cache[:, 1].reshape(BATCH_SEQUENCES, N_SEQ, CACHED_PER_INDEX, KEY_VALUE_HEADS, HEAD_SIZE).astype(jnp.float32)
    scores = jnp.einsum('bgrd,bjtgd->bgrjt', query_rows_local, stored_keys) * inv_root
    position = jnp.arange(CTX, dtype=jnp.int32).reshape(N_SEQ, CACHED_PER_INDEX)
    is_valid = (position[None] < lengths[:, None, None])[:, None, None]
    masked = jnp.where(is_valid, scores, NEGATIVE)
    block_max = lax.optimization_barrier(jnp.max(masked, axis=4))
    weights = jnp.where(is_valid, jnp.exp(masked - block_max[..., None]), 0.0)
    block_sum = lax.optimization_barrier(jnp.sum(weights, axis=4))
    block_out = jnp.einsum('bgrjt,bjtgd->bgrjd', rounded(weights), stored_values)
    new_score = jnp.einsum('bgrd,bgd->bgr', query_rows_local, new_key) * inv_root
    top_score = jnp.maximum(lax.optimization_barrier(jnp.max(block_max, axis=3)), new_score)
    block_rescale = jnp.exp(block_max - top_score[..., None])
    new_weight = jnp.exp(new_score - top_score)
    denominator = lax.optimization_barrier(jnp.sum(block_sum * block_rescale, axis=3)) + new_weight
    numerator = lax.optimization_barrier(jnp.sum(block_out * block_rescale[..., None], axis=3)) + new_weight[..., None] * new_value[:, :, None, :]
    attended = (numerator / denominator[..., None]).astype(jnp.bfloat16).reshape(BATCH_SEQUENCES, QUERY_HEADS * HEAD_SIZE)
    attn_out = jnp.dot(attended, w_output, preferred_element_type=jnp.float32)
    hidden_mid = (hidden_wide + attn_out).astype(jnp.bfloat16)
    mid_wide = hidden_mid.astype(jnp.float32)
    inv_second = lax.rsqrt(lax.optimization_barrier(jnp.mean(mid_wide * mid_wide, axis=1)) + EPSILON)
    scaled_mid = (mid_wide * mamba_gain).astype(jnp.bfloat16)
    projected = jnp.dot(scaled_mid, w_inproj.reshape(MODEL_WIDTH, 2 * DI), preferred_element_type=jnp.float32).reshape(BATCH_SEQUENCES, 2, DI)
    conv_input = (inv_second[:, None] * projected[:, 0]).astype(jnp.bfloat16)
    gate_part = inv_second[:, None] * projected[:, 1]
    window = jnp.concatenate([conv_window, conv_input[:, None, :]], axis=1)
    conv_out = conv_bias + lax.optimization_barrier(jnp.sum(conv_weight[None] * window.astype(jnp.float32), axis=1))
    conv_act = jax.nn.silu(conv_out).astype(jnp.bfloat16)
    xproj_out = jnp.dot(conv_act, w_xproj, preferred_element_type=jnp.float32)
    rate_low = xproj_out[:, :DTR].astype(jnp.bfloat16)
    input_proj = xproj_out[:, DTR:DTR + DS]
    output_proj = xproj_out[:, DTR + DS:]
    step_size = jax.nn.softplus(jnp.dot(rate_low, w_dtproj, preferred_element_type=jnp.float32) + dt_bias)
    decays = jnp.exp(-step_size[:, None, :] * jnp.exp(a_log)[None])
    conv_wide = conv_act.astype(jnp.float32)
    state_out = decays * ssm_state + step_size[:, None, :] * input_proj[:, :, None] * conv_wide[:, None, :]
    readout = lax.optimization_barrier(jnp.sum(output_proj[:, :, None] * state_out, axis=1)) + d_skip * conv_wide
    gated_out = (readout * jax.nn.silu(gate_part)).astype(jnp.bfloat16)
    mamba_out = jnp.dot(gated_out, w_outproj, preferred_element_type=jnp.float32)
    hidden_out = (mid_wide + mamba_out).astype(jnp.bfloat16)
    return (hidden_out, state_out, window[:, 1:])
```

```python
import functools

import jax
import jax.numpy as jnp
from jax import lax
from jax.experimental import pallas as pl
from jax.experimental.pallas import tpu as pltpu
from jax.sharding import PartitionSpec as P

MODEL_WIDTH = 8192
QUERY_HEADS = 64
KEY_VALUE_HEADS = 8
HEAD_SIZE = 128
DS = 16
DTR = 512


EPSILON = 1e-06
NEGATIVE = -1e30


def joined(value, axis, join):
    pieces = jax.tree.map(lambda part: lax.all_gather(part, axis), value)
    head = jax.tree.map(lambda part: part[0], pieces)
    tail = jax.tree.map(lambda part: part[1:], pieces)
    subtotal, _ = lax.scan(lambda subtotal, piece: (join(subtotal, piece), None), head, tail)
    return subtotal


def combine_parts(earlier, later):
    first_max, first_sum, first_out = earlier
    second_max, second_sum, second_out = later
    largest = jnp.maximum(first_max, second_max)
    first_factor = jnp.exp(first_max - largest)
    second_factor = jnp.exp(second_max - largest)
    return (
        largest,
        first_sum * first_factor + second_sum * second_factor,
        first_out * first_factor[..., None] + second_out * second_factor[..., None],
    )


def plain_on_device(
    hidden_in,
    lengths,
    key_value_cache,
    attn_gain,
    w_query,
    key_value_weight,
    w_output,
    mamba_gain,
    w_inproj,
    conv_weight,
    conv_bias,
    w_xproj,
    w_dtproj,
    dt_bias,
    a_log,
    d_skip,
    w_outproj,
    ssm_state,
    conv_window,
):
    batch = hidden_in.shape[0]
    seq_index = lax.axis_index("seq")
    query_groups_count = QUERY_HEADS // KEY_VALUE_HEADS
    local_kv = key_value_weight.shape[2] // HEAD_SIZE
    head_cols = local_kv * query_groups_count * HEAD_SIZE
    gathered = lax.all_gather(hidden_in, ("section", "tp"), axis=1, tiled=True)
    wide_in = gathered.astype(jnp.float32)
    normed_input = (wide_in * attn_gain).astype(jnp.bfloat16)
    square_part = jnp.sum(wide_in * wide_in, axis=1)
    query_part = jnp.dot(normed_input, w_query, preferred_element_type=jnp.float32)
    keyval_part = jnp.dot(
        normed_input,
        key_value_weight.reshape(key_value_weight.shape[0], 2 * key_value_weight.shape[2]),
        preferred_element_type=jnp.float32,
    )
    square_sum, query_sum, keyval_sum = lax.psum((square_part, query_part, keyval_part), "seq")
    reciprocal_leading = lax.rsqrt(square_sum / MODEL_WIDTH + EPSILON)
    query_rows_local = (
        (reciprocal_leading[:, None] * query_sum)
        .astype(jnp.bfloat16)
        .reshape(batch, local_kv, query_groups_count, HEAD_SIZE)
    )
    key_value_rows = (
        (reciprocal_leading[:, None] * keyval_sum)
        .astype(jnp.bfloat16)
        .reshape(batch, 2, local_kv, HEAD_SIZE)
    )
    new_key = key_value_rows[:, 0]
    new_value = key_value_rows[:, 1]
    span = key_value_cache.shape[2]
    stored_keys = key_value_cache[:, 0].reshape(batch, span, local_kv, HEAD_SIZE)
    stored_values = key_value_cache[:, 1].reshape(batch, span, local_kv, HEAD_SIZE)
    inv_root = HEAD_SIZE ** (-0.5)
    scores = (
        jnp.einsum(
            "bgrd,btgd->bgrt", query_rows_local, stored_keys, preferred_element_type=jnp.float32
        )
        * inv_root
    )
    position = seq_index * span + jnp.arange(span, dtype=jnp.int32)
    is_valid = (position[None, :] < lengths[:, None])[:, None, None, :]
    masked = jnp.where(is_valid, scores, NEGATIVE)
    local_max = jnp.max(masked, axis=3)
    weights = jnp.where(is_valid, jnp.exp(masked - local_max[..., None]), 0.0)
    local_sum = jnp.sum(weights, axis=3)
    local_out = jnp.einsum(
        "bgrt,btgd->bgrd",
        weights.astype(jnp.bfloat16),
        stored_values,
        preferred_element_type=jnp.float32,
    )
    new_score = (
        jnp.einsum("bgrd,bgd->bgr", query_rows_local, new_key, preferred_element_type=jnp.float32)
        * inv_root
    )
    value_wide = jnp.broadcast_to(
        new_value[:, :, None, :], (batch, local_kv, query_groups_count, HEAD_SIZE)
    ).astype(jnp.float32)
    new_part = (new_score, jnp.ones_like(new_score), value_wide)
    merged = joined((local_max, local_sum, local_out), "seq", combine_parts)
    top_score, denominator, numerator = combine_parts(merged, new_part)
    attended = (numerator / denominator[..., None]).astype(jnp.bfloat16).reshape(batch, head_cols)
    attn_part = jnp.dot(attended, w_output, preferred_element_type=jnp.float32)
    attn_piece = lax.psum_scatter(attn_part, ("section", "tp"), scatter_dimension=1, tiled=True)
    hidden_mid = (hidden_in.astype(jnp.float32) + attn_piece).astype(jnp.bfloat16)
    mid_rows = lax.all_gather(hidden_mid, ("section", "tp"), axis=1, tiled=True)
    mid_wide = mid_rows.astype(jnp.float32)
    mid_square = lax.psum(jnp.sum(mid_wide * mid_wide, axis=1), "seq")
    inv_second = lax.rsqrt(mid_square / MODEL_WIDTH + EPSILON)
    scaled_mid = (mid_wide * mamba_gain).astype(jnp.bfloat16)
    in_rows = w_inproj.shape[0]
    local_inner = w_inproj.shape[2]
    both_term = jnp.dot(
        scaled_mid, w_inproj.reshape(in_rows, 2 * local_inner), preferred_element_type=jnp.float32
    ).reshape(batch, 2, local_inner)
    both_sum = lax.psum_scatter(both_term, "seq", scatter_dimension=2, tiled=True)
    conv_sum = both_sum[:, 0]
    gate_sum = both_sum[:, 1]
    conv_input = (inv_second[:, None] * conv_sum).astype(jnp.bfloat16)
    window = jnp.concatenate([conv_window, conv_input[:, None, :]], axis=1)
    conv_out = conv_bias + jnp.sum(conv_weight[None] * window.astype(jnp.float32), axis=1)
    conv_act = jax.nn.silu(conv_out).astype(jnp.bfloat16)
    xproj_out = lax.psum(
        jnp.dot(conv_act, w_xproj, preferred_element_type=jnp.float32), ("seq", "section", "tp")
    )
    rate_low = xproj_out[:, :DTR].astype(jnp.bfloat16)
    input_proj = xproj_out[:, DTR : DTR + DS]
    output_proj = xproj_out[:, DTR + DS :]
    step_size = jax.nn.softplus(
        jnp.dot(rate_low, w_dtproj, preferred_element_type=jnp.float32) + dt_bias
    )
    decays = jnp.exp(-step_size[:, None, :] * jnp.exp(a_log)[None])
    conv_wide = conv_act.astype(jnp.float32)
    state_out = (
        decays * ssm_state + step_size[:, None, :] * input_proj[:, :, None] * conv_wide[:, None, :]
    )
    readout = jnp.sum(output_proj[:, :, None] * state_out, axis=1) + d_skip * conv_wide
    gate_part = inv_second[:, None] * gate_sum
    gated_out = (readout * jax.nn.silu(gate_part)).astype(jnp.bfloat16)
    mamba_part = jnp.dot(
        lax.all_gather(gated_out, "seq", axis=1, tiled=True),
        w_outproj,
        preferred_element_type=jnp.float32,
    )
    mamba_piece = lax.psum_scatter(mamba_part, ("section", "tp"), scatter_dimension=1, tiled=True)
    hidden_out = (hidden_mid.astype(jnp.float32) + mamba_piece).astype(jnp.bfloat16)
    return (hidden_out, state_out, window[:, 1:])


LANES = 128
F32 = jnp.float32
BF16 = jnp.bfloat16
VMEM = pl.BlockSpec(memory_space=pltpu.VMEM)
HBM = pl.BlockSpec(memory_space=pltpu.HBM)


def swap(value, axis, count, distance):
    return lax.ppermute(value, axis, [(index, index ^ distance) for index in range(count)])


def exchange(value, axis, count):
    return [swap(value, axis, count, distance) for distance in range(1, count)]


def tree_sum(parts):
    parts = list(parts)
    while len(parts) > 1:
        parts = [parts[i] + parts[i + 1] for i in range(0, len(parts), 2)]
    return parts[0]


def call(kernel, outs, args, name, specs=None, scratch=(), limit=6, flops=0, moved=0):
    return pl.pallas_call(
        kernel,
        out_shape=tuple(pltpu.VMEM(shape, dtype) for shape, dtype in outs),
        in_specs=[VMEM] * len(args) if specs is None else specs,
        out_specs=tuple(VMEM for _ in outs),
        scratch_shapes=list(scratch),
        compiler_params=pltpu.CompilerParams(vmem_limit_bytes=limit << 20),
        cost_estimate=pl.CostEstimate(flops=flops, bytes_accessed=moved, transcendentals=0),
        name=name,
    )(*args)


def resident(value):
    return pltpu.with_memory_space_constraint(value, pltpu.VMEM)


def fetch_pairs(weight, chunks, first, name):
    rows = weight.shape[0]

    def kernel(w_ref, o_ref, sem):
        base = first()
        copies = [
            pltpu.make_async_copy(w_ref.at[:, base + j], o_ref.at[j], sem.at[j])
            for j in range(chunks)
        ]
        for copy in copies:
            copy.start()
        for copy in copies:
            copy.wait()

    (held,) = call(
        kernel,
        [((chunks, rows, 2, LANES), BF16)],
        [pltpu.with_memory_space_constraint(weight, pltpu.HBM)],
        name,
        specs=[HBM],
        scratch=[pltpu.SemaphoreType.DMA((chunks,))],
        limit=1,
        moved=2 * 2 * rows * chunks * 2 * LANES,
    )
    return held.reshape(chunks, 2 * rows, LANES)


def paired_view(weight):
    rows, two, columns = weight.shape
    return weight.reshape(rows, two, columns // LANES, LANES).transpose(0, 2, 1, 3)


def expand_rows(value, out_ref):
    rows, depth = value.shape
    count = depth // LANES
    k = lax.broadcasted_iota(jnp.int32, (LANES, 4 * LANES), 0)
    lane = lax.broadcasted_iota(jnp.int32, (LANES, 4 * LANES), 1)
    hit = (lane == 2 * k) | (lane == 2 * LANES + 2 * k + 1)
    spread = jnp.where(hit, 1.0, 0.0).astype(BF16)
    wide = value.astype(F32)
    stacked = jnp.concatenate(
        [wide[:, m * LANES : (m + 1) * LANES] for m in range(count)], axis=0
    ).astype(BF16)
    both = jnp.dot(stacked, spread, preferred_element_type=F32)
    for m in range(count):
        block = both[m * rows : (m + 1) * rows]
        out_ref[:, m * 2 * LANES : (m + 1) * 2 * LANES] = jnp.concatenate(
            [block[:, : 2 * LANES], block[:, 2 * LANES :]], axis=0
        ).astype(BF16)


def split3(value):
    high = value.astype(BF16).astype(F32)
    rest = value - high
    mid = rest.astype(BF16).astype(F32)
    low = (rest - mid).astype(BF16).astype(F32)
    return high, mid, low


def on_device(
    mesh,
    hidden_in,
    lengths,
    key_value_cache,
    attn_gain,
    w_query,
    key_value_weight,
    w_output,
    mamba_gain,
    w_inproj,
    conv_weight,
    conv_bias,
    w_xproj,
    w_dtproj,
    dt_bias,
    a_log,
    d_skip,
    w_outproj,
    ssm_state,
    conv_window,
):
    n_seq = mesh.shape["seq"]
    n_tp = mesh.shape["tp"]
    n_col = mesh.shape["section"] * n_tp
    columns_axis = ("section", "tp")
    batch, piece = hidden_in.shape
    rows_in = w_query.shape[0]
    head_cols = w_query.shape[1]
    kv_cols = key_value_weight.shape[2]
    span = key_value_cache.shape[2]
    mid_cols = w_output.shape[1]
    inner = w_inproj.shape[2]
    channels = ssm_state.shape[2]
    low = w_xproj.shape[1]
    regular = (
        batch == 8
        and n_seq in (1, 2, 4)
        and n_col in (1, 2, 4)
        and span == LANES
        and kv_cols % (2 * LANES) == 0
        and channels % (2 * LANES) == 0
        and piece % LANES == 0
    )
    if not regular:
        return plain_on_device(
            hidden_in,
            lengths,
            key_value_cache,
            attn_gain,
            w_query,
            key_value_weight,
            w_output,
            mamba_gain,
            w_inproj,
            conv_weight,
            conv_bias,
            w_xproj,
            w_dtproj,
            dt_bias,
            a_log,
            d_skip,
            w_outproj,
            ssm_state,
            conv_window,
        )

    ratio = QUERY_HEADS // KEY_VALUE_HEADS
    local_kv = kv_cols // HEAD_SIZE
    heads = local_kv * ratio
    inv_root = HEAD_SIZE ** (-0.5)
    stats = 2 * heads

    def seq_place():
        return lax.axis_index("seq")

    def col_place():
        return lax.axis_index("section") * n_tp + lax.axis_index("tp")

    def offset(index, size):
        return pl.multiple_of(index * size, size)

    with jax.named_scope("gather_in"):
        in_parts = [hidden_in] + exchange(hidden_in, columns_axis, n_col)

    def query_kernel(*refs):
        parts, (gain_ref, w_ref, q_ref, x_ref, normed_ref) = refs[:n_col], refs[n_col:]
        me = col_place()
        total = None
        square = None
        for k in range(n_col):
            at = offset(me ^ k, piece)
            raw = parts[k][...]
            wide = raw.astype(F32)
            normed = (wide * gain_ref[:, pl.ds(at, piece)]).astype(BF16)
            x_ref[:, pl.ds(at, piece)] = raw
            normed_ref[:, pl.ds(at, piece)] = normed
            part = jnp.dot(normed, w_ref[pl.ds(at, piece), :], preferred_element_type=F32)
            total = part if total is None else total + part
            s = jnp.sum(wide * wide, axis=1, keepdims=True)
            square = s if square is None else square + s
        q_ref[:, :head_cols] = total
        q_ref[:, head_cols:] = jnp.broadcast_to(square, (batch, LANES))

    query_msg, x_full, normed = call(
        query_kernel,
        [((batch, head_cols + LANES), F32), ((batch, rows_in), BF16), ((batch, rows_in), BF16)],
        in_parts + [attn_gain.reshape(1, rows_in), resident(w_query)],
        "query",
        flops=2 * batch * rows_in * head_cols,
        moved=2 * rows_in * head_cols,
    )
    with jax.named_scope("sum_query"):
        query_parts = [query_msg] + exchange(query_msg, "seq", n_seq)

    kv_held = fetch_pairs(paired_view(key_value_weight), kv_cols // LANES, lambda: 0, "fetch_kv")
    in_view = paired_view(w_inproj)
    per_seq = channels // LANES
    in_held = [
        fetch_pairs(
            in_view, per_seq, lambda k=k: (seq_place() ^ k) * per_seq, "fetch_in" + str(k)
        )
        for k in range(n_seq)
    ]

    def kv_kernel(normed_ref, w_ref, kv_ref, wide_ref):
        expand_rows(normed_ref[...], wide_ref)
        for j in range(0, kv_cols // LANES, 2):
            w = jnp.concatenate([w_ref[j], w_ref[j + 1]], axis=1)
            out = jnp.dot(wide_ref[...], w, preferred_element_type=F32)
            kv_ref[:, j * LANES : (j + 2) * LANES] = out[:batch].astype(BF16)
            kv_ref[:, kv_cols + j * LANES : kv_cols + (j + 2) * LANES] = out[batch:].astype(BF16)

    (kv_part,) = call(
        kv_kernel,
        [((batch, 2 * kv_cols), BF16)],
        [normed, kv_held],
        "key_value",
        scratch=[pltpu.VMEM((2 * batch, 2 * rows_in), BF16)],
        flops=4 * batch * rows_in * kv_cols,
        moved=4 * rows_in * kv_cols,
    )

    length_rows = jnp.broadcast_to(lengths[:, None], (batch, LANES))
    rows_of_group = ratio * batch

    def attend_kernel(*refs):
        parts = refs[:n_seq]
        kv_ref, cache_ref, len_ref, msg_ref, q_ref, inv_ref = refs[n_seq:]
        square = tree_sum([p[:, head_cols:] for p in parts])
        inv = lax.rsqrt(square / MODEL_WIDTH + EPSILON)
        inv_ref[...] = inv
        inv_col = inv[:, :1]
        query = (inv_col * tree_sum([p[:, :head_cols] for p in parts])).astype(BF16)
        q_ref[...] = query
        wide_query = query.astype(F32)
        row = lax.broadcasted_iota(jnp.int32, (rows_of_group, LANES), 0) % batch
        position = seq_place() * span + lax.broadcasted_iota(jnp.int32, (batch, LANES), 1)
        valid = position < len_ref[...]
        valid = jnp.concatenate([valid.astype(F32)] * ratio, axis=0) > 0.5
        lane = lax.broadcasted_iota(jnp.int32, (batch, LANES), 1)
        table = jnp.zeros((batch, LANES), F32)
        for g in range(local_kv):
            cols = slice(g * HEAD_SIZE, (g + 1) * HEAD_SIZE)
            group = jnp.concatenate(
                [
                    wide_query[:, (g * ratio + r) * HEAD_SIZE : (g * ratio + r + 1) * HEAD_SIZE]
                    for r in range(ratio)
                ],
                axis=0,
            ).astype(BF16)
            scores = jnp.zeros((rows_of_group, LANES), F32)
            for b in range(batch):
                s = lax.dot_general(
                    group,
                    cache_ref[b, 0, :, cols],
                    (((1,), (1,)), ((), ())),
                    preferred_element_type=F32,
                )
                scores = jnp.where(row == b, s, scores)
            masked = jnp.where(valid, scores * inv_root, NEGATIVE)
            top = jnp.max(masked, axis=1, keepdims=True)
            weights = jnp.where(valid, jnp.exp(masked - top), 0.0)
            total = jnp.sum(weights, axis=1, keepdims=True)
            rounded = weights.astype(BF16)
            out = jnp.zeros((rows_of_group, HEAD_SIZE), F32)
            for b in range(batch):
                o = jnp.dot(rounded, cache_ref[b, 1, :, cols], preferred_element_type=F32)
                out = jnp.where(row == b, o, out)
            for r in range(ratio):
                h = g * ratio + r
                rows = slice(r * batch, (r + 1) * batch)
                msg_ref[:, h * HEAD_SIZE : (h + 1) * HEAD_SIZE] = out[rows].astype(BF16)
                table = jnp.where(lane == h, top[rows], table)
                table = jnp.where(lane == heads + h, total[rows], table)
        high, mid, rest = split3(table)
        packed = jnp.where(lane < stats, high, 0.0)
        packed = packed + jnp.where(
            (lane >= stats) & (lane < 2 * stats), pltpu.roll(mid, stats, 1), 0.0
        )
        packed = packed + jnp.where(
            (lane >= 2 * stats) & (lane < 3 * stats), pltpu.roll(rest, 2 * stats, 1), 0.0
        )
        msg_ref[:, head_cols : head_cols + 2 * kv_cols] = kv_ref[...]
        msg_ref[:, head_cols + 2 * kv_cols :] = packed.astype(BF16)

    msg_cols = head_cols + 2 * kv_cols + LANES
    attend_msg, query, inv_first = call(
        attend_kernel,
        [((batch, msg_cols), BF16), ((batch, head_cols), BF16), ((batch, LANES), F32)],
        query_parts + [kv_part, resident(key_value_cache), length_rows],
        "attend",
        flops=8 * batch * batch * heads * span * HEAD_SIZE,
        moved=4 * batch * span * kv_cols,
    )
    with jax.named_scope("join_softmax"):
        attend_parts = [attend_msg] + exchange(attend_msg, "seq", n_seq)

    def output_kernel(*refs):
        parts = refs[:n_seq]
        q_ref, inv_ref, w_ref, out_ref, att_ref = refs[n_seq:]
        inv_col = inv_ref[:, :1]
        kv_sum = tree_sum([p[:, head_cols : head_cols + 2 * kv_cols].astype(F32) for p in parts])
        kv_new = (inv_col * kv_sum).astype(BF16).astype(F32)
        lane = lax.broadcasted_iota(jnp.int32, (batch, LANES), 1)
        tables = []
        for p in parts:
            packed = p[:, head_cols + 2 * kv_cols :].astype(F32)
            tables.append(
                packed
                + pltpu.roll(packed, LANES - stats, 1)
                + pltpu.roll(packed, LANES - 2 * stats, 1)
            )
        tops = tables
        sums = [pltpu.roll(t, LANES - heads, 1) for t in tables]
        new_score = jnp.zeros((batch, LANES), F32)
        for h in range(heads):
            g = h // ratio
            q = q_ref[:, h * HEAD_SIZE : (h + 1) * HEAD_SIZE].astype(F32)
            k = kv_new[:, g * HEAD_SIZE : (g + 1) * HEAD_SIZE]
            s = jnp.sum(q * k, axis=1, keepdims=True) * inv_root
            new_score = jnp.where(lane == h, s, new_score)
        used = lane < heads
        tops = [jnp.where(used, t, 0.0) for t in tops]
        top = new_score
        for t in tops:
            top = jnp.maximum(top, t)
        factors = [jnp.exp(t - top) for t in tops]
        new_factor = jnp.exp(new_score - top)
        bottom = tree_sum([f * s for f, s in zip(factors, sums)]) + new_factor
        bottom = jnp.where(used, bottom, 1.0)
        factors = [f / bottom for f in factors]
        new_factor = new_factor / bottom
        for h in range(heads):
            g = h // ratio
            cols = slice(h * HEAD_SIZE, (h + 1) * HEAD_SIZE)
            value = kv_new[:, kv_cols + g * HEAD_SIZE : kv_cols + (g + 1) * HEAD_SIZE]
            mixed = tree_sum([f[:, h : h + 1] * p[:, cols].astype(F32) for f, p in zip(factors, parts)])
            att_ref[:, cols] = (mixed + new_factor[:, h : h + 1] * value).astype(BF16)
        out_ref[...] = jnp.dot(att_ref[...], w_ref[...], preferred_element_type=F32).astype(BF16)

    (attn_msg,) = call(
        output_kernel,
        [((batch, mid_cols), BF16)],
        attend_parts + [query, inv_first, resident(w_output)],
        "output",
        scratch=[pltpu.VMEM((batch, head_cols), BF16)],
        flops=2 * batch * head_cols * mid_cols,
        moved=2 * head_cols * mid_cols,
    )
    with jax.named_scope("sum_attention"):
        attn_parts = [attn_msg] + exchange(attn_msg, columns_axis, n_col)

    def inproj_kernel(*refs):
        parts = refs[:n_col]
        x_ref, gain_ref = refs[n_col : n_col + 2]
        w_refs = refs[n_col + 2 : n_col + 2 + n_seq]
        own_ref = refs[n_col + 2 + n_seq]
        msg_refs = refs[n_col + 3 + n_seq : n_col + 3 + 2 * n_seq]
        mid_ref, wide_ref = refs[n_col + 3 + 2 * n_seq :]
        mid = x_ref[...].astype(F32) + tree_sum([p[...].astype(F32) for p in parts])
        mid = mid.astype(BF16)
        mid_ref[...] = mid
        own_ref[...] = mid_ref[:, pl.ds(offset(col_place(), piece), piece)]
        wide = mid.astype(F32)
        square = jnp.sum(wide * wide, axis=1, keepdims=True)
        expand_rows((wide * gain_ref[...]).astype(BF16), wide_ref)
        high = square.astype(BF16).astype(F32)
        both = jnp.concatenate([high, square - high], axis=0)
        both = jnp.broadcast_to(both, (2 * batch, LANES)).astype(BF16)
        for w_ref, msg_ref in zip(w_refs, msg_refs):
            for j in range(0, per_seq, 2):
                w = jnp.concatenate([w_ref[j], w_ref[j + 1]], axis=1)
                out = jnp.dot(wide_ref[...], w, preferred_element_type=F32)
                msg_ref[:, j * LANES : (j + 2) * LANES] = out.astype(BF16)
            msg_ref[:, channels:] = both

    outs = call(
        inproj_kernel,
        [((batch, piece), BF16)] + [((2 * batch, channels + LANES), BF16)] * n_seq,
        attn_parts + [x_full, mamba_gain.reshape(1, rows_in)] + in_held,
        "inproj",
        scratch=[pltpu.VMEM((batch, rows_in), BF16), pltpu.VMEM((2 * batch, 2 * rows_in), BF16)],
        flops=8 * batch * rows_in * inner,
        moved=4 * rows_in * inner,
    )
    mid_own, both_msgs = outs[0], outs[1:]
    with jax.named_scope("sum_inproj"):
        both_parts = [both_msgs[0]] + [
            swap(both_msgs[k], "seq", n_seq, k) for k in range(1, n_seq)
        ]

    taps = conv_weight.shape[0]
    conv_base = conv_bias + jnp.sum(
        conv_weight[None, : taps - 1] * conv_window.astype(F32), axis=1
    )
    last_tap = conv_weight[taps - 1 :]

    def conv_kernel(*refs):
        parts = refs[:n_seq]
        base_ref, tap_ref, w_ref, in_ref, act_ref, gate_ref, low_ref = refs[n_seq:]
        square = tree_sum([p[:batch, channels:].astype(F32) + p[batch:, channels:].astype(F32) for p in parts])
        inv = lax.rsqrt(square[:, :1] / MODEL_WIDTH + EPSILON)
        both = tree_sum([p[:, :channels].astype(F32) for p in parts])
        conv_in = (inv * both[:batch]).astype(BF16)
        in_ref[...] = conv_in
        conv_out = base_ref[...] + tap_ref[...] * conv_in.astype(F32)
        act = jax.nn.silu(conv_out).astype(BF16)
        act_ref[...] = act
        gate_ref[...] = jax.nn.silu(inv * both[batch:])
        low_ref[...] = jnp.dot(act, w_ref[...], preferred_element_type=F32)

    conv_in, conv_act, gate_act, low_part = call(
        conv_kernel,
        [
            ((batch, channels), BF16),
            ((batch, channels), BF16),
            ((batch, channels), F32),
            ((batch, low), F32),
        ],
        both_parts + [conv_base, last_tap, resident(w_xproj)],
        "conv",
        flops=2 * batch * channels * low,
        moved=2 * channels * low,
    )
    with jax.named_scope("sum_xproj"):
        low_sum = tree_sum([low_part] + exchange(low_part, columns_axis, n_col))
        low_parts = [low_sum] + exchange(low_sum, "seq", n_seq)

    def state_kernel(*refs):
        parts = refs[:n_seq]
        w_ref, bias_ref, a_ref, skip_ref, act_ref, gate_ref, st_ref = refs[n_seq : n_seq + 7]
        new_ref, gated_ref, read_ref = refs[n_seq + 7 :]
        total = tree_sum([p[...] for p in parts])
        rate = total[:, :DTR].astype(BF16)
        proj = total[:, DTR:]
        step = jax.nn.softplus(
            jnp.dot(rate, w_ref[...], preferred_element_type=F32) + bias_ref[...]
        )
        decay = -jnp.exp(a_ref[...])
        act = act_ref[...].astype(F32)
        driven = step * act
        width = 2 * DS
        lane = lax.broadcasted_iota(jnp.int32, (DS, width), 1)
        row = lax.broadcasted_iota(jnp.int32, (DS, width), 0)
        for b in range(batch):
            line = jnp.broadcast_to(proj[b : b + 1], (DS, width))
            column_in = jnp.sum(jnp.where(lane == row, line, 0.0), axis=1, keepdims=True)
            column_out = jnp.sum(jnp.where(lane == row + DS, line, 0.0), axis=1, keepdims=True)
            new = jnp.exp(step[b : b + 1] * decay) * st_ref[b] + column_in * driven[b : b + 1]
            new_ref[b] = new
            read_ref[b : b + 1, :] = jnp.sum(column_out * new, axis=0, keepdims=True)
        gated_ref[...] = (
            (read_ref[...] + skip_ref[...] * act) * gate_ref[...]
        ).astype(BF16)

    state_out, gated = call(
        state_kernel,
        [((batch, DS, channels), F32), ((batch, channels), BF16)],
        low_parts
        + [
            resident(w_dtproj),
            dt_bias.reshape(1, channels),
            resident(a_log),
            d_skip.reshape(1, channels),
            conv_act,
            gate_act,
            resident(ssm_state),
        ],
        "state",
        scratch=[pltpu.VMEM((batch, channels), F32)],
        flops=2 * batch * DTR * channels,
        moved=2 * DTR * channels,
    )
    with jax.named_scope("gather_gated"):
        gated_parts = [gated] + exchange(gated, "seq", n_seq)

    def outproj_kernel(*refs):
        parts = refs[:n_seq]
        w_ref = refs[n_seq]
        out_refs = refs[n_seq + 1 :]
        me, place = col_place(), seq_place()
        for k in range(n_col):
            cols = pl.ds(offset(me ^ k, piece), piece)
            total = tree_sum(
                [
                    jnp.dot(
                        parts[j][...],
                        w_ref[pl.ds(offset(place ^ j, channels), channels), cols],
                        preferred_element_type=F32,
                    )
                    for j in range(n_seq)
                ]
            )
            out_refs[k][...] = total.astype(BF16)

    out_msgs = call(
        outproj_kernel,
        [((batch, piece), BF16)] * n_col,
        gated_parts + [resident(w_outproj)],
        "outproj",
        flops=2 * batch * n_seq * channels * mid_cols,
        moved=2 * n_seq * channels * mid_cols,
    )
    with jax.named_scope("sum_outproj"):
        out_parts = [out_msgs[0]] + [
            swap(out_msgs[k], columns_axis, n_col, k) for k in range(1, n_col)
        ]
    hidden_out = (
        mid_own.astype(F32) + tree_sum([p.astype(F32) for p in out_parts])
    ).astype(BF16)
    window_out = jnp.concatenate([conv_window[:, 1:], conv_in[:, None, :]], axis=1)
    return (hidden_out, state_out, window_out)


def solution(mesh):
    return jax.shard_map(
        functools.partial(on_device, mesh),
        mesh=mesh,
        in_specs=(
            P("groups", ("seq", "section", "tp")),
            P("groups"),
            P("groups", None, "seq", ("section", "tp")),
            P("seq"),
            P("seq", ("section", "tp")),
            P("seq", None, ("section", "tp")),
            P(("section", "tp"), "seq"),
            P("seq"),
            P("seq", None, ("section", "tp")),
            P(None, ("section", "tp", "seq")),
            P(("section", "tp", "seq")),
            P(("section", "tp", "seq"), None),
            P(None, ("section", "tp", "seq")),
            P(("section", "tp", "seq")),
            P(None, ("section", "tp", "seq")),
            P(("section", "tp", "seq")),
            P(("section", "tp"), "seq"),
            P("groups", None, ("section", "tp", "seq")),
            P("groups", None, ("section", "tp", "seq")),
        ),
        out_specs=(
            P("groups", ("seq", "section", "tp")),
            P("groups", None, ("section", "tp", "seq")),
            P("groups", None, ("section", "tp", "seq")),
        ),
        check_vma=False,
    )
```
